32 devices in a mesh: pages: 8 (over z, core), blocks: 4 (over y, x).
Axes of the slice: x: 2, y: 2, z: 4, core: 2. Of those that a mesh axis runs over, the one named last changes fastest.
Arguments:
- queries: bfloat16 [64, 24, 128], P(('pages', 'blocks')), may hold values from -0.5 to 0.5
- centroids: bfloat16 [256, 128], replicated, may hold values from -6 to 6
- basis: bfloat16 [256, 32, 128], replicated, may hold values from -1 to 1
- patch_ids: int32 [8, 32, 256], P('pages', None, 'blocks'), may hold values from 0 to 255
- coeffs: bfloat16 [8, 32, 8192], P('pages', None, 'blocks'), may hold values from -6 to 6
- page_counts: int32 [8, 32], P('pages'), may hold values from 128 to 256
- cand_ids: int32 [8, 64, 16], P('pages'), may hold values from 0 to 31
- cand_counts: int32 [8, 64], P('pages'), may hold values from 0 to 16, as said below
Outputs:
- scores: float32 [64, 8, 16], P(('pages', 'blocks'))
The draws below stay inside these ranges and needn't reach their ends.
Inputs may be any that keep to these rules, and one draw needn't show every extreme that they name: `cand_ids`: slots at or past a query's count in a group are padding and name arbitrary pages; ids may repeat. `cand_counts`: each query's counts over the 8 groups add up to 64.
All inputs are finite; a program needn't handle non-finite values.
Results may differ from the reference program's by a relative error of at most 0.00065.
Values may be sent and summed in bfloat16 or wider, within the bound.
A program may use at most 64 MiB of HBM per device.

```python
import jax
import jax.numpy as jnp
from jax import lax

DIM = 128
QTOK = 24
RANK = 32
NCENT = 256
CANDS = 64
PAGES_GRP = 32
NGROUPS = 8
NQ = 64
CMAX = 16
PATCHES = 256


def draw_page_counts(key, part):
    counts = jax.random.randint(key, (NGROUPS, PAGES_GRP), PATCHES // 2, PATCHES + 1)
    return counts.at[0, 0].set(PATCHES)


def draw_cand_counts(key, part):
    even_share = CANDS // NGROUPS
    key_heat, key_pair, key_move = jax.random.split(key, 3)
    heat_rank = jax.random.permutation(key_heat, NGROUPS)
    pairing = jax.vmap(lambda subkey: jax.random.permutation(subkey, NGROUPS))(jax.random.split(key_pair, NQ))
    pair_left = pairing[:, 0::2]
    pair_right = pairing[:, 1::2]
    moved_count = even_share - jax.random.randint(key_move, (NQ, NGROUPS // 2), 0, even_share // 4 + 1)
    moved_count = moved_count.at[0, 0].set(even_share)
    left_hot = heat_rank[pair_left] > heat_rank[pair_right]
    winner_group = jnp.where(left_hot, pair_left, pair_right)
    loser_group = jnp.where(left_hot, pair_right, pair_left)
    row_index = jnp.arange(NQ)[:, None]
    counts = jnp.zeros((NQ, NGROUPS), jnp.int32)
    counts = counts.at[row_index, winner_group].set(even_share + moved_count)
    counts = counts.at[row_index, loser_group].set(even_share - moved_count)
    return counts.T


def touch_ends(values, rng, low, high):
    spot = [jax.random.randint(jax.random.fold_in(rng, axis), (), 0, length) for axis, length in enumerate(values.shape)]
    widest = values.shape.index(max(values.shape))
    next_to = spot[:widest] + [(spot[widest] + 1) % values.shape[widest]] + spot[widest + 1:]
    return values.at[tuple(spot)].set(low).at[tuple(next_to)].set(high)


def level_of(key, shape, cuts, smallest, top_value):
    loudness, own = 1.0, jax.random.fold_in(key, 6)
    for dim, parts in cuts:
        steps = jnp.exp(jax.random.uniform(jax.random.fold_in(own, dim), (parts,), jnp.float32, smallest / len(cuts), top_value / len(cuts)))
        loudness = loudness * jnp.repeat(steps, shape[dim] // parts).reshape([-1 if axis == dim else 1 for axis in range(len(shape))])
    return loudness


def centred(key, extent, deviation, reach, shards=(), held_as=jnp.bfloat16):
    drawn = jax.random.normal(key, extent, jnp.float32) * deviation
    if len(shards) > 0:
        drawn = level_of(key, extent, shards, -0.22, 0.18) * drawn
    return jnp.clip(drawn, min=-reach, max=reach).astype(held_as)


def setup_inputs(seed: int = 0) -> dict:
    splits = jax.random.split(jax.random.key(seed), 9)
    return {
        "queries": centred(splits[0], (NQ, QTOK, DIM), DIM ** -0.5, 0.5, ((0, 32),)),
        "centroids": centred(splits[1], (NCENT, DIM), 1.0, 6.0),
        "basis": centred(splits[2], (NCENT, RANK, DIM), RANK ** -0.5, 1.0),
        "patch_ids": touch_ends(jax.random.randint(splits[3], (NGROUPS, PAGES_GRP, PATCHES), 0, NCENT), jax.random.fold_in(splits[3], 1), 0, NCENT - 1).astype(jnp.int32),
        "coeffs": centred(splits[4], (NGROUPS, PAGES_GRP, PATCHES * RANK), 1.0, 6.0, ((0, 8), (2, 4))),
        "page_counts": draw_page_counts(jax.random.fold_in(splits[8], 71), 0),
        "cand_ids": touch_ends(jax.random.randint(splits[6], (NGROUPS, NQ, CMAX), 0, PAGES_GRP), jax.random.fold_in(splits[6], 1), 0, PAGES_GRP - 1).astype(jnp.int32),
        "cand_counts": draw_cand_counts(jax.random.fold_in(splits[8], 71), 0),
    }


def decode_group(group_ids, group_coef, centroids, basis):
    def one_page(inputs):
        page_ids, page_coef = inputs
        center = centroids[page_ids].astype(jnp.float32)
        chosen = basis[page_ids].astype(jnp.float32)
        coeff_rows = page_coef.reshape(PATCHES, RANK).astype(jnp.float32)
        residual = jnp.einsum("nj,njd->nd", coeff_rows, chosen)
        return (center + residual).astype(jnp.bfloat16)
    return lax.map(one_page, (group_ids, group_coef))


def score_group(group_emb, group_live, group_cands, group_counts, queries):
    patch_pos = jnp.arange(PATCHES, dtype=jnp.int32)
    slot_pos = jnp.arange(CMAX, dtype=jnp.int32)

    def one_block(inputs):
        query_group, cand_group, count_group = inputs
        chosen = group_emb[cand_group].astype(jnp.float32)
        similar = jnp.einsum("gcpd,gtd->gcpt", chosen, query_group.astype(jnp.float32))
        valid_patch = patch_pos[None, None, :] < group_live[cand_group][:, :, None]
        similar = jnp.where(valid_patch[..., None], similar, -jnp.inf)
        block_best = jnp.max(similar, axis=2)
        slot_used = slot_pos[None, :] < count_group[:, None]
        return jnp.where(slot_used[..., None], block_best, 0.0).astype(jnp.bfloat16)

    blocks = NQ // 16
    results = lax.map(one_block, (queries.reshape(blocks, 16, QTOK, DIM), group_cands.reshape(blocks, 16, CMAX), group_counts.reshape(blocks, 16)))
    return results.reshape(NQ, CMAX, QTOK)


def reference(queries, centroids, basis, patch_ids, coeffs, page_counts, cand_ids, cand_counts):
    def per_group(inputs):
        group_ids, group_coef, group_live, group_cands, group_counts = inputs
        group_emb = decode_group(group_ids, group_coef, centroids, basis)
        return score_group(group_emb, group_live, group_cands, group_counts, queries)

    block_best = lax.map(per_group, (patch_ids, coeffs, page_counts, cand_ids, cand_counts))
    scores = jnp.sum(block_best.astype(jnp.float32), axis=3) / QTOK
    return jnp.transpose(scores, (1, 0, 2))
```

```python
import functools

import jax
import jax.numpy as jnp
from jax import lax
from jax.experimental import pallas as pl
from jax.experimental.pallas import tpu as pltpu
from jax.sharding import PartitionSpec as P

MESH = pl.DeviceIdType.MESH
SPLIT = 2
STEP = 8
LOWEST = -3.0e38


def remote(src, dst, send, recv, where):
    return pltpu.make_async_remote_copy(
        src_ref=src, dst_ref=dst, send_sem=send, recv_sem=recv, device_id=where, device_id_type=MESH
    )


def kernel(
    n_pages, n_blocks, qtok,
    q_hbm, cent_hbm, basis_hbm, ids_hbm, coef_hbm, count_hbm, cand_hbm, live_hbm, out_ref,
    cent, basis, ids, coef, count, cand, live,
    qbuf, idb, dlow, emb, first, bound, outgo, income, scoreT, piece, landed,
    in_sem, z_send, z_recv, b_send, b_recv, c_send, c_recv, d_send, d_recv, e_send, e_recv,
):
    k = lax.axis_index("pages")
    r = lax.axis_index("blocks")
    core = lax.rem(k, 2)
    z = lax.div(k, 2)
    nz = n_pages // 2
    pages, patches = ids.shape
    cents, width = cent.shape
    rank = basis.shape[0] // cents
    rows_q = q_hbm.shape[0]
    cols = n_pages * rows_q

    barrier = pltpu.get_barrier_semaphore()
    for s in range(1, n_pages):
        pl.semaphore_signal(
            barrier, inc=1, device_id=(lax.rem(k + s, n_pages), r), device_id_type=MESH
        )
    for s in range(1, n_blocks):
        pl.semaphore_signal(
            barrier, inc=1, device_id=(k, lax.rem(r + s, n_blocks)), device_id_type=MESH
        )

    own = qbuf.at[r, core, pl.ds(pl.multiple_of(z * rows_q, rows_q), rows_q), :]
    loads = [
        pltpu.make_async_copy(src, dst, in_sem.at[i])
        for i, (src, dst) in enumerate(
            [
                (ids_hbm, ids), (count_hbm, count), (q_hbm, own), (coef_hbm, coef),
                (cent_hbm, cent), (basis_hbm, basis), (cand_hbm, cand), (live_hbm, live),
            ]
        )
    ]
    for copy in loads:
        copy.start()

    loads[0].wait()
    loads[1].wait()
    low_total = cents // SPLIT
    lane = lax.broadcasted_iota(jnp.int32, (pages, width), 1)
    lane_cent = lax.div(lane, rank)
    for p in range(patches):
        wide = jnp.broadcast_to(ids[:, p : p + 1], (pages, width))
        idb[p] = wide.astype(jnp.float32).astype(jnp.bfloat16)
        dlow[p] = (
            (lax.bitwise_and(wide, low_total - 1) - lane_cent).astype(jnp.float32).astype(jnp.bfloat16)
        )
    spread = jnp.broadcast_to(count[...].astype(jnp.float32), (pages, pages))
    diag = lax.broadcasted_iota(jnp.int32, (pages, pages), 0) == lax.broadcasted_iota(
        jnp.int32, (pages, pages), 1
    )
    column = jnp.sum(jnp.where(diag, spread, 0.0), axis=1, keepdims=True)
    bound[...] = jnp.broadcast_to(column, (pages, width)) - (r * patches).astype(jnp.float32)

    loads[2].wait()
    pl.semaphore_wait(barrier, n_pages - 1 + n_blocks - 1)
    z_copies = []
    for s in range(1, nz):
        to = lax.rem(z + s, nz)
        z_copies.append(
            remote(own, own, z_send.at[s], z_recv.at[s], (to * 2 + core, r))
        )
    for copy in z_copies:
        copy.start()

    for copy in loads[3:]:
        copy.wait()

    per = width // rank
    tile_row = lax.broadcasted_iota(jnp.int32, (width, per * width), 0)
    tile_col = lax.broadcasted_iota(jnp.int32, (width, per * width), 1)
    tile = (
        (tile_row == lax.div(tile_col, width) * rank + lax.rem(tile_col, rank))
        .astype(jnp.float32)
        .astype(jnp.bfloat16)
    )
    depth = low_total * rank
    rows = STEP * pages

    def decode(m):
        base = m * STEP
        parts = []
        for h in range(STEP // per):
            chunk = coef[:, pl.ds(pl.multiple_of((m * (STEP // per) + h) * width, width), width)]
            spreadc = jnp.dot(chunk, tile, preferred_element_type=jnp.float32)
            for s in range(per):
                parts.append(spreadc[:, s * width : (s + 1) * width].astype(jnp.bfloat16))
        weights = jnp.concatenate(parts, axis=0)
        low = dlow[pl.ds(base, STEP)].reshape(rows, width)
        mine = idb[pl.ds(base, STEP)].reshape(rows, width)
        zero = jnp.zeros((rows, width), jnp.bfloat16)
        lhs = jnp.concatenate(
            [
                jnp.where(low == jnp.bfloat16(per * t), weights, zero)
                for t in range(depth // width)
            ],
            axis=1,
        )
        rhs = jnp.concatenate(
            [basis[h * depth : (h + 1) * depth, :] for h in range(SPLIT)], axis=1
        )
        res = jnp.dot(lhs, rhs, preferred_element_type=jnp.float32)
        lane_id = lax.broadcasted_iota(jnp.int32, (rows, width), 1).astype(jnp.float32).astype(jnp.bfloat16)
        one = jnp.ones((rows, width), jnp.bfloat16)
        hot = jnp.concatenate(
            [
                jnp.where(mine == lane_id + jnp.bfloat16(t * width), one, zero)
                for t in range(cents // width)
            ],
            axis=1,
        )
        center = jnp.dot(hot, cent[...], preferred_element_type=jnp.float32)
        mine_f = mine.astype(jnp.float32)
        total = res[:, :width]
        for h in range(1, SPLIT):
            total = jnp.where(
                mine_f >= float(h * low_total), res[:, h * width : (h + 1) * width], total
            )
        total = (total + center).reshape(STEP, pages, width)

        @pl.when(m == 0)
        def _():
            first[...] = total[0]

        position = base + lax.broadcasted_iota(jnp.int32, (STEP, pages, width), 0)
        valid = position.astype(jnp.float32) < bound[...][None]
        total = jnp.where(valid, total, first[...][None])
        emb[pl.ds(pl.multiple_of(m * rows, rows), rows), :] = total.astype(jnp.bfloat16).reshape(rows, width)

    turns = patches // STEP
    half = turns // 2

    def decode_step(m, carry):
        decode(m)
        return carry

    lax.fori_loop(0, half, decode_step, 0)

    partner = (k + 1 - 2 * core, r)
    for copy in z_copies:
        copy.wait_recv()
    b_copies = []
    for s in range(1, n_blocks):
        to = lax.rem(r + s, n_blocks)
        b_copies.append(
            remote(qbuf.at[r, core], qbuf.at[r, core], b_send.at[s], b_recv.at[s], (k, to))
        )
    for copy in b_copies:
        copy.start()
    c_copies = [
        remote(qbuf.at[r, core], qbuf.at[r, core], c_send.at[0], c_recv.at[0], partner)
    ]
    c_copies[0].start()

    lax.fori_loop(half, turns, decode_step, 0)

    for s in range(1, n_blocks):
        b_copies[s - 1].wait_recv()
        source = lax.rem(r + n_blocks - s, n_blocks)
        copy = remote(
            qbuf.at[source, core], qbuf.at[source, core], c_send.at[s], c_recv.at[s], partner
        )
        copy.start()
        c_copies.append(copy)

    def best_of(source):
        query = qbuf[source].reshape(cols, width)

        def more(m, best):
            block = emb[pl.ds(pl.multiple_of(m * rows, rows), rows), :]
            sim = lax.dot_general(
                block, query, (((1,), (1,)), ((), ())), preferred_element_type=jnp.float32
            )
            return jnp.maximum(best, jnp.max(sim.reshape(STEP, pages, cols), axis=0))

        best = lax.fori_loop(0, turns, more, jnp.full((pages, cols), LOWEST, jnp.float32))
        return jnp.where(bound[:, :1] > 0.0, best, LOWEST).astype(jnp.bfloat16)

    d_copies = []
    for s in range(n_blocks):
        c_copies[s].wait_recv()
        source = lax.rem(r + n_blocks - s, n_blocks)
        if s == 0:
            income[0] = best_of(source)
        else:
            outgo[s] = best_of(source)
            copy = remote(outgo.at[s], income.at[s], d_send.at[s], d_recv.at[s], (k, source))
            copy.start()
            d_copies.append(copy)

    n_query = cand.shape[1]
    per_dev = rows_q // qtok
    spot = lax.broadcasted_iota(jnp.int32, (cols, n_query), 0)
    seen = lax.broadcasted_iota(jnp.int32, (cols, n_query), 1)
    shard = lax.div(spot, rows_q)
    owner = lax.rem(shard, nz) * 2 + lax.div(shard, nz)
    index = (owner * n_blocks + r) * per_dev + lax.div(lax.rem(spot, rows_q), qtok)
    gather = (index == seen).astype(jnp.float32).astype(jnp.bfloat16)
    slots = cand.shape[0]
    used = lax.broadcasted_iota(jnp.int32, (slots, n_query), 0) < live[...]
    chosen = cand[...]

    highest = income[0].astype(jnp.float32)
    for copy in d_copies:
        copy.wait_recv()
    for s in range(1, n_blocks):
        highest = jnp.maximum(highest, income[s].astype(jnp.float32))
    sums = jnp.dot(highest.astype(jnp.bfloat16), gather, preferred_element_type=jnp.float32)
    picked = jnp.zeros((slots, n_query), jnp.float32)
    for n in range(pages):
        picked = jnp.where(chosen == n, sums[n : n + 1, :], picked)
    picked = jnp.where(used, picked / qtok, 0.0)
    wide_q = scoreT.shape[0]
    padded = picked
    if wide_q > n_query:
        padded = jnp.concatenate([padded, jnp.zeros((slots, wide_q - n_query), jnp.float32)], axis=1)
    full = jnp.concatenate([padded, jnp.zeros((width - slots, wide_q), jnp.float32)], axis=0)
    scoreT[...] = full.T

    e_copies = []
    for s in range(n_pages):
        to = lax.rem(k + s, n_pages)
        values = scoreT[pl.ds((to * n_blocks + r) * per_dev, per_dev), :]
        if s == 0:
            landed[k] = values
        else:
            piece[s] = values
            copy = remote(piece.at[s], landed.at[k], e_send.at[s], e_recv.at[s], (to, r))
            copy.start()
            e_copies.append(copy)
    for copy in e_copies:
        copy.wait_recv()
    for g in range(n_pages):
        arrived = landed[g]
        for i in range(per_dev):
            out_ref[i, g : g + 1, :] = arrived[i : i + 1, :slots]
    for copy in z_copies + b_copies + c_copies + d_copies + e_copies:
        copy.wait_send()


def on_device(queries, centroids, basis, patch_ids, coeffs, page_counts, cand_ids, cand_counts):
    n_pages = lax.axis_size("pages")
    n_blocks = lax.axis_size("blocks")
    owned, qtok, width = queries.shape
    cents, rank, _ = basis.shape
    _, pages, patches = patch_ids.shape
    _, n_query, slots = cand_ids.shape
    rows_q = owned * qtok
    cols = n_pages * rows_q
    args = (
        queries.reshape(rows_q, width),
        centroids,
        basis.reshape(cents * rank, width),
        patch_ids[0],
        coeffs[0],
        page_counts,
        jnp.swapaxes(cand_ids[0], 0, 1),
        cand_counts,
    )
    dma = pltpu.SemaphoreType.DMA
    bf16, f32 = jnp.bfloat16, jnp.float32
    vmem = pltpu.VMEM
    return pl.pallas_call(
        functools.partial(kernel, n_pages, n_blocks, qtok),
        out_shape=jax.ShapeDtypeStruct((owned, n_pages, slots), f32),
        in_specs=[pl.BlockSpec(memory_space=pl.ANY)] * len(args),
        out_specs=pl.BlockSpec(memory_space=pltpu.VMEM),
        scratch_shapes=[vmem(a.shape, a.dtype) for a in args[1:]]
        + [
            vmem((n_blocks, 2, cols // 2, width), bf16),
            vmem((patches, pages, width), bf16),
            vmem((patches, pages, width), bf16),
            vmem((patches * pages, width), bf16),
            vmem((pages, width), f32),
            vmem((pages, width), f32),
            vmem((n_blocks, pages, cols), bf16),
            vmem((n_blocks, pages, cols), bf16),
            vmem((-(-n_query // 128) * 128, width), f32),
            vmem((n_pages, owned, width), f32),
            vmem((n_pages, owned, width), f32),
            dma((len(args),)),
            dma((n_pages,)), dma((n_pages,)),
            dma((n_blocks,)), dma((n_blocks,)),
            dma((n_blocks,)), dma((n_blocks,)),
            dma((n_blocks,)), dma((n_blocks,)),
            dma((n_pages,)), dma((n_pages,)),
        ],
        compiler_params=pltpu.CompilerParams(collective_id=0, has_side_effects=True),
    )(*args)


def solution(mesh):
    placed = (
        P(("pages", "blocks"), None, None),
        P(),
        P(),
        P("pages", None, "blocks"),
        P("pages", None, "blocks"),
        P("pages", None),
        P("pages", None, None),
        P("pages", None),
    )
    return jax.shard_map(
        on_device,
        mesh=mesh,
        in_specs=placed,
        out_specs=P(("pages", "blocks"), None, None),
        check_vma=False,
    )
```

```python
import functools

import jax
import jax.numpy as jnp
from jax import lax
from jax.experimental import pallas as pl
from jax.experimental.pallas import tpu as pltpu
from jax.sharding import PartitionSpec as P

MESH = pl.DeviceIdType.MESH
SPLIT = 4
STEP = 8
AHEAD, NEAR, FAR = 1, 3, 4
LOWEST = -3.0e38


def remote(src, dst, send, recv, where):
    return pltpu.make_async_remote_copy(
        src_ref=src, dst_ref=dst, send_sem=send, recv_sem=recv, device_id=where, device_id_type=MESH
    )


def flip(index, bits):
    for bit in range(bits.bit_length()):
        if bits >> bit & 1:
            index = index + 2**bit - 2 ** (bit + 1) * lax.rem(lax.div(index, 2**bit), 2)
    return index


def far_first(count):
    return sorted(range(1, count), key=lambda s: -s.bit_count())


def kernel(
    n_pages, n_blocks, qtok,
    q_hbm, cent_hbm, basis_hbm, ids_hbm, coef_hbm, count_hbm, cand_hbm, live_hbm, out_ref,
    cent, basis, ids, coef, count, cand, live,
    qbuf, idb, dlow, emb, first, bound, outgo, income, gather, scoreT, piece, landed,
    in_sem, z_send, z_recv, b_send, b_recv, c_send, c_recv, d_send, d_recv, e_send, e_recv,
):
    k = lax.axis_index("pages")
    r = lax.axis_index("blocks")
    core = lax.rem(k, 2)
    z = lax.div(k, 2)
    nz = n_pages // 2
    pages, patches = ids.shape
    cents, width = cent.shape
    rank = basis.shape[0] // cents
    rows_q = q_hbm.shape[0]
    cols = n_pages * rows_q

    barrier = pltpu.get_barrier_semaphore()
    for s in range(1, n_pages):
        pl.semaphore_signal(
            barrier, inc=1, device_id=(lax.rem(k + s, n_pages), r), device_id_type=MESH
        )
    for s in range(1, n_blocks):
        pl.semaphore_signal(
            barrier, inc=1, device_id=(k, lax.rem(r + s, n_blocks)), device_id_type=MESH
        )

    own = qbuf.at[r, core, pl.ds(pl.multiple_of(z * rows_q, rows_q), rows_q), :]
    loads = [
        pltpu.make_async_copy(src, dst, in_sem.at[i])
        for i, (src, dst) in enumerate(
            [
                (ids_hbm, ids), (count_hbm, count), (q_hbm, own), (coef_hbm, coef),
                (cent_hbm, cent), (basis_hbm, basis), (cand_hbm, cand), (live_hbm, live),
            ]
        )
    ]
    for copy in loads:
        copy.start()

    loads[0].wait()
    loads[1].wait()
    low_total = cents // SPLIT
    lane_cent = lax.div(lax.broadcasted_iota(jnp.int32, (pages, STEP * width), 1), rank)
    lane_cent = lax.rem(lane_cent, width // rank).astype(jnp.float32)
    id_f = ids[...].astype(jnp.float32)
    id_low = lax.bitwise_and(ids[...], low_total - 1).astype(jnp.float32)
    id_both = jnp.concatenate([id_f, id_low], axis=0).astype(jnp.bfloat16)
    from_row = lax.broadcasted_iota(jnp.int32, (patches, STEP * width), 0)
    to_col = lax.div(lax.broadcasted_iota(jnp.int32, (patches, STEP * width), 1), width)
    for m in range(patches // STEP):
        pick = (from_row == to_col + m * STEP).astype(jnp.float32).astype(jnp.bfloat16)
        wide = jnp.dot(id_both, pick, preferred_element_type=jnp.float32)
        wide_id = wide[:pages].astype(jnp.bfloat16)
        wide_low = (wide[pages:] - lane_cent).astype(jnp.bfloat16)
        for p in range(STEP):
            idb[m * STEP + p] = wide_id[:, p * width : (p + 1) * width]
            dlow[m * STEP + p] = wide_low[:, p * width : (p + 1) * width]
    spread = jnp.broadcast_to(count[...].astype(jnp.float32), (pages, pages))
    diag = lax.broadcasted_iota(jnp.int32, (pages, pages), 0) == lax.broadcasted_iota(
        jnp.int32, (pages, pages), 1
    )
    column = jnp.sum(jnp.where(diag, spread, 0.0), axis=1, keepdims=True)
    bound[...] = jnp.broadcast_to(column, (pages, width)) - (r * patches).astype(jnp.float32)

    for copy in loads[3:]:
        copy.wait()

    n_query = cand.shape[1]
    per_dev = rows_q // qtok
    spot = lax.broadcasted_iota(jnp.int32, (cols, n_query), 0)
    seen = lax.broadcasted_iota(jnp.int32, (cols, n_query), 1)
    shard = lax.div(spot, rows_q)
    owner = lax.rem(shard, nz) * 2 + lax.div(shard, nz)
    index = (owner * n_blocks + r) * per_dev + lax.div(lax.rem(spot, rows_q), qtok)
    gather[...] = (index == seen).astype(jnp.float32).astype(jnp.bfloat16)

    per = width // rank
    tile_row = lax.broadcasted_iota(jnp.int32, (width, per * width), 0)
    tile_col = lax.broadcasted_iota(jnp.int32, (width, per * width), 1)
    tile = (
        (tile_row == lax.div(tile_col, width) * rank + lax.rem(tile_col, rank))
        .astype(jnp.float32)
        .astype(jnp.bfloat16)
    )
    depth = low_total * rank
    rows = STEP * pages

    def decode(m):
        base = m * STEP
        parts = []
        for h in range(STEP // per):
            chunk = coef[:, pl.ds(pl.multiple_of((m * (STEP // per) + h) * width, width), width)]
            spreadc = jnp.dot(chunk, tile, preferred_element_type=jnp.float32)
            for s in range(per):
                parts.append(spreadc[:, s * width : (s + 1) * width].astype(jnp.bfloat16))
        weights = jnp.concatenate(parts, axis=0)
        low = dlow[pl.ds(base, STEP)].reshape(rows, width)
        mine = idb[pl.ds(base, STEP)].reshape(rows, width)
        zero = jnp.zeros((rows, width), jnp.bfloat16)
        lhs = jnp.concatenate(
            [
                jnp.where(low == jnp.bfloat16(per * t), weights, zero)
                for t in range(depth // width)
            ],
            axis=1,
        )
        rhs = jnp.concatenate(
            [basis[h * depth : (h + 1) * depth, :] for h in range(SPLIT)], axis=1
        )
        res = jnp.dot(lhs, rhs, preferred_element_type=jnp.float32)
        lane_id = lax.broadcasted_iota(jnp.int32, (rows, width), 1).astype(jnp.float32).astype(jnp.bfloat16)
        one = jnp.ones((rows, width), jnp.bfloat16)
        hot = jnp.concatenate(
            [
                jnp.where(mine == lane_id + jnp.bfloat16(t * width), one, zero)
                for t in range(cents // width)
            ],
            axis=1,
        )
        center = jnp.dot(hot, cent[...], preferred_element_type=jnp.float32)
        mine_f = mine.astype(jnp.float32)
        total = res[:, :width]
        for h in range(1, SPLIT):
            total = jnp.where(
                mine_f >= float(h * low_total), res[:, h * width : (h + 1) * width], total
            )
        total = (total + center).reshape(STEP, pages, width)

        @pl.when(m == 0)
        def _():
            first[...] = total[0]

        position = base + lax.broadcasted_iota(jnp.int32, (STEP, pages, width), 0)
        valid = position.astype(jnp.float32) < bound[...][None]
        total = jnp.where(valid, total, first[...][None])
        emb[pl.ds(pl.multiple_of(m * rows, rows), rows), :] = total.astype(jnp.bfloat16).reshape(rows, width)

    turns = patches // STEP

    def decode_steps(start, stop):
        start, stop = min(start, turns), min(stop, turns)
        if stop > start:
            lax.fori_loop(start, stop, lambda m, carry: (decode(m), carry)[1], 0)

    def shard_at(block, where):
        return qbuf.at[block, core, pl.ds(pl.multiple_of(where * rows_q, rows_q), rows_q), :]

    decode_steps(0, AHEAD)
    loads[2].wait()
    pl.semaphore_wait(barrier, n_pages - 1 + n_blocks - 1)
    z_copies = {
        s: remote(own, own, z_send.at[s], z_recv.at[s], (flip(z, s) * 2 + core, r))
        for s in far_first(nz)
    }
    for copy in z_copies.values():
        copy.start()
    b_copies = {}

    def forward(t):
        if t:
            z_copies[t].wait_recv()
        part = shard_at(r, flip(z, t))
        for s in far_first(n_blocks):
            b_copies[s, t] = remote(
                part, part, b_send.at[s, t], b_recv.at[s, t], (k, flip(r, s))
            )
            b_copies[s, t].start()

    forward(0)
    decode_steps(AHEAD, NEAR)
    for t in range(1, nz // 2 + 1):
        forward(t)
    decode_steps(NEAR, FAR)
    for t in range(nz // 2 + 1, nz):
        forward(t)
    partner = (k + 1 - 2 * core, r)

    def share(s):
        for t in range(nz):
            if s:
                b_copies[s, t].wait_recv()
        half = qbuf.at[flip(r, s), core]
        copy = remote(half, half, c_send.at[s], c_recv.at[s], partner)
        copy.start()
        return copy

    c_copies = {0: share(0)}
    decode_steps(FAR, turns)

    def best_of(source):
        query = qbuf[source].reshape(cols, width)

        best = jnp.full((pages, cols), LOWEST, jnp.float32)
        for m in range(turns):
            sim = lax.dot_general(
                emb[m * rows : (m + 1) * rows, :], query, (((1,), (1,)), ((), ())),
                preferred_element_type=jnp.float32,
            )
            best = jnp.maximum(best, jnp.max(sim.reshape(STEP, pages, cols), axis=0))
        return jnp.where(bound[:, :1] > 0.0, best, LOWEST).astype(jnp.bfloat16)

    c_copies[0].wait_recv()
    income[0] = best_of(r)
    for s in far_first(n_blocks):
        c_copies[s] = share(s)
    d_copies = []
    for s in far_first(n_blocks):
        c_copies[s].wait_recv()
        source = flip(r, s)
        outgo[s] = best_of(source)
        copy = remote(outgo.at[s], income.at[s], d_send.at[s], d_recv.at[s], (k, source))
        copy.start()
        d_copies.append(copy)

    slots = cand.shape[0]
    used = lax.broadcasted_iota(jnp.int32, (slots, n_query), 0) < live[...]
    chosen = cand[...]

    highest = income[0].astype(jnp.float32)
    for copy in d_copies:
        copy.wait_recv()
    for s in range(1, n_blocks):
        highest = jnp.maximum(highest, income[s].astype(jnp.float32))
    sums = jnp.dot(highest.astype(jnp.bfloat16), gather[...], preferred_element_type=jnp.float32)
    picked = jnp.zeros((slots, n_query), jnp.float32)
    for n in range(pages):
        picked = jnp.where(chosen == n, sums[n : n + 1, :], picked)
    picked = jnp.where(used, picked, 0.0)
    wide_q = scoreT.shape[0]
    padded = picked
    if wide_q > n_query:
        padded = jnp.concatenate([padded, jnp.zeros((slots, wide_q - n_query), jnp.float32)], axis=1)
    full = jnp.concatenate([padded, jnp.zeros((width - slots, wide_q), jnp.float32)], axis=0)
    scoreT[...] = full.T

    e_copies = []
    for s in range(n_pages - 1, -1, -1):
        to = flip(k, s)
        values = scoreT[pl.ds((to * n_blocks + r) * per_dev, per_dev), :]
        if s == 0:
            landed[k] = values
        else:
            piece[s] = values
            copy = remote(piece.at[s], landed.at[k], e_send.at[s], e_recv.at[s], (to, r))
            copy.start()
            e_copies.append(copy)
    for copy in e_copies:
        copy.wait_recv()
    for g in range(n_pages):
        arrived = landed[g]
        for i in range(per_dev):
            out_ref[i, g : g + 1, :] = arrived[i : i + 1, :slots]
    started = [*z_copies.values(), *b_copies.values(), *c_copies.values(), *d_copies, *e_copies]
    for copy in started:
        copy.wait_send()


def on_device(queries, centroids, basis, patch_ids, coeffs, page_counts, cand_ids, cand_counts):
    n_pages = lax.axis_size("pages")
    n_blocks = lax.axis_size("blocks")
    owned, qtok, width = queries.shape
    cents, rank, _ = basis.shape
    _, pages, patches = patch_ids.shape
    _, n_query, slots = cand_ids.shape
    rows_q = owned * qtok
    cols = n_pages * rows_q
    args = (
        queries.reshape(rows_q, width),
        centroids,
        basis.reshape(cents * rank, width),
        patch_ids[0],
        coeffs[0],
        page_counts,
        jnp.swapaxes(cand_ids[0], 0, 1),
        cand_counts,
    )
    dma = pltpu.SemaphoreType.DMA
    bf16, f32 = jnp.bfloat16, jnp.float32
    vmem = pltpu.VMEM
    totals = pl.pallas_call(
        functools.partial(kernel, n_pages, n_blocks, qtok),
        out_shape=jax.ShapeDtypeStruct((owned, n_pages, slots), f32),
        in_specs=[pl.BlockSpec(memory_space=pl.ANY)] * len(args),
        out_specs=pl.BlockSpec(memory_space=pltpu.VMEM),
        scratch_shapes=[vmem(a.shape, a.dtype) for a in args[1:]]
        + [
            vmem((n_blocks, 2, cols // 2, width), bf16),
            vmem((patches, pages, width), bf16),
            vmem((patches, pages, width), bf16),
            vmem((patches * pages, width), bf16),
            vmem((pages, width), f32),
            vmem((pages, width), f32),
            vmem((n_blocks, pages, cols), bf16),
            vmem((n_blocks, pages, cols), bf16),
            vmem((cols, n_query), bf16),
            vmem((-(-n_query // 128) * 128, width), f32),
            vmem((n_pages, owned, width), f32),
            vmem((n_pages, owned, width), f32),
            dma((len(args),)),
            dma((n_pages,)), dma((n_pages,)),
            dma((n_blocks, n_pages // 2)), dma((n_blocks, n_pages // 2)),
            dma((n_blocks,)), dma((n_blocks,)),
            dma((n_blocks,)), dma((n_blocks,)),
            dma((n_pages,)), dma((n_pages,)),
        ],
        compiler_params=pltpu.CompilerParams(collective_id=0, has_side_effects=True),
    )(*args)
    return totals / qtok


def solution(mesh):
    placed = (
        P(("pages", "blocks"), None, None),
        P(),
        P(),
        P("pages", None, "blocks"),
        P("pages", None, "blocks"),
        P("pages", None),
        P("pages", None, None),
        P("pages", None),
    )
    return jax.shard_map(
        on_device,
        mesh=mesh,
        in_specs=placed,
        out_specs=P(("pages", "blocks"), None, None),
        check_vma=False,
    )
```

```python
import functools

import jax
import jax.numpy as jnp
from jax import lax
from jax.experimental import pallas as pl
from jax.experimental.pallas import tpu as pltpu
from jax.sharding import PartitionSpec as P

MESH = pl.DeviceIdType.MESH
SPLIT = 4
STEP = 8
AHEAD, NEAR, FAR = 1, 3, 4
LOWEST = -3.0e38


def remote(src, dst, send, recv, where):
    return pltpu.make_async_remote_copy(
        src_ref=src, dst_ref=dst, send_sem=send, recv_sem=recv, device_id=where, device_id_type=MESH
    )


def flip(index, bits):
    for bit in range(bits.bit_length()):
        if bits >> bit & 1:
            index = index + 2**bit - 2 ** (bit + 1) * lax.rem(lax.div(index, 2**bit), 2)
    return index


def far_first(count):
    return sorted(range(1, count), key=lambda s: -s.bit_count())


def kernel(
    n_pages, n_blocks, qtok,
    q_hbm, cent_hbm, basis_hbm, ids_hbm, coef_hbm, count_hbm, cand_hbm, live_hbm, out_ref,
    cent, basis, ids, coef, count, cand, live,
    qbuf, idb, dlow, emb, first, bound, outgo, income, gather, scoreT, piece, landed,
    in_sem, z_send, z_recv, b_send, b_recv, c_send, c_recv, d_send, d_recv, e_send, e_recv,
):
    k = lax.axis_index("pages")
    r = lax.axis_index("blocks")
    core = lax.rem(k, 2)
    z = lax.div(k, 2)
    nz = n_pages // 2
    pages, patches = ids.shape
    cents, width = cent.shape
    rank = basis.shape[0] // cents
    rows_q = q_hbm.shape[0]
    cols = n_pages * rows_q

    barrier = pltpu.get_barrier_semaphore()
    for s in range(1, n_pages):
        pl.semaphore_signal(
            barrier, inc=1, device_id=(lax.rem(k + s, n_pages), r), device_id_type=MESH
        )
    for s in range(1, n_blocks):
        pl.semaphore_signal(
            barrier, inc=1, device_id=(k, lax.rem(r + s, n_blocks)), device_id_type=MESH
        )

    own = qbuf.at[r, core, pl.ds(pl.multiple_of(z * rows_q, rows_q), rows_q), :]
    loads = [
        pltpu.make_async_copy(src, dst, in_sem.at[i])
        for i, (src, dst) in enumerate(
            [
                (ids_hbm, ids), (count_hbm, count), (q_hbm, own), (coef_hbm, coef),
                (cent_hbm, cent), (basis_hbm, basis), (cand_hbm, cand), (live_hbm, live),
            ]
        )
    ]
    for copy in loads:
        copy.start()

    loads[0].wait()
    loads[1].wait()
    low_total = cents // SPLIT
    lane_cent = lax.div(lax.broadcasted_iota(jnp.int32, (1, STEP * width), 1), rank)
    lane_cent = lax.rem(lane_cent, width // rank).astype(jnp.float32)
    id_f = ids[...].astype(jnp.float32)
    id_low = lax.bitwise_and(ids[...], low_total - 1).astype(jnp.float32)
    id_both = jnp.concatenate([id_f, id_low], axis=0).astype(jnp.bfloat16)
    to_col = lax.div(lax.broadcasted_iota(jnp.int32, (1, STEP * width), 1), width)
    from_row = lax.broadcasted_iota(jnp.int32, (STEP, STEP * width), 0)
    pick = (from_row == to_col).astype(jnp.float32).astype(jnp.bfloat16)
    for m in range(patches // STEP):
        wide = jnp.dot(
            id_both[:, m * STEP : (m + 1) * STEP], pick, preferred_element_type=jnp.float32
        )
        wide_id = wide[:pages].astype(jnp.bfloat16)
        wide_low = (wide[pages:] - lane_cent).astype(jnp.bfloat16)
        for p in range(STEP):
            idb[m * STEP + p] = wide_id[:, p * width : (p + 1) * width]
            dlow[m * STEP + p] = wide_low[:, p * width : (p + 1) * width]
    spread = jnp.broadcast_to(count[...].astype(jnp.float32), (pages, pages))
    diag = lax.broadcasted_iota(jnp.int32, (pages, pages), 0) == lax.broadcasted_iota(
        jnp.int32, (pages, pages), 1
    )
    column = jnp.sum(jnp.where(diag, spread, 0.0), axis=1, keepdims=True)
    bound[...] = jnp.broadcast_to(column, (pages, width)) - (r * patches).astype(jnp.float32)

    for copy in loads[3:]:
        copy.wait()

    n_query = cand.shape[1]
    per_dev = rows_q // qtok
    spot = lax.broadcasted_iota(jnp.int32, (1, cols), 1)
    seen = lax.broadcasted_iota(jnp.int32, (n_query, cols), 0)
    shard = lax.div(spot, rows_q)
    owner = lax.rem(shard, nz) * 2 + lax.div(shard, nz)
    index = (owner * n_blocks + r) * per_dev + lax.div(lax.rem(spot, rows_q), qtok)
    gather[...] = (index == seen).astype(jnp.float32).astype(jnp.bfloat16)

    per = width // rank
    tile_row = lax.broadcasted_iota(jnp.int32, (width, per * width), 0)
    tile_col = lax.broadcasted_iota(jnp.int32, (1, per * width), 1)
    tile = (
        (tile_row == lax.div(tile_col, width) * rank + lax.rem(tile_col, rank))
        .astype(jnp.float32)
        .astype(jnp.bfloat16)
    )
    depth = low_total * rank
    rows = STEP * pages

    def decode(m):
        base = m * STEP
        parts = []
        for h in range(STEP // per):
            chunk = coef[:, pl.ds(pl.multiple_of((m * (STEP // per) + h) * width, width), width)]
            spreadc = jnp.dot(chunk, tile, preferred_element_type=jnp.float32)
            for s in range(per):
                parts.append(spreadc[:, s * width : (s + 1) * width].astype(jnp.bfloat16))
        weights = jnp.concatenate(parts, axis=0)
        low = dlow[pl.ds(base, STEP)].reshape(rows, width)
        mine = idb[pl.ds(base, STEP)].reshape(rows, width)
        zero = jnp.zeros((rows, width), jnp.bfloat16)
        lhs = jnp.concatenate(
            [
                jnp.where(low == jnp.bfloat16(per * t), weights, zero)
                for t in range(depth // width)
            ],
            axis=1,
        )
        rhs = jnp.concatenate(
            [basis[h * depth : (h + 1) * depth, :] for h in range(SPLIT)], axis=1
        )
        res = jnp.dot(lhs, rhs, preferred_element_type=jnp.float32)
        lane_id = lax.broadcasted_iota(jnp.int32, (rows, width), 1).astype(jnp.float32).astype(jnp.bfloat16)
        one = jnp.ones((rows, width), jnp.bfloat16)
        hot = jnp.concatenate(
            [
                jnp.where(mine == lane_id + jnp.bfloat16(t * width), one, zero)
                for t in range(cents // width)
            ],
            axis=1,
        )
        center = jnp.dot(hot, cent[...], preferred_element_type=jnp.float32)
        mine_f = mine.astype(jnp.float32)
        total = res[:, :width]
        for h in range(1, SPLIT):
            total = jnp.where(
                mine_f >= float(h * low_total), res[:, h * width : (h + 1) * width], total
            )
        total = (total + center).reshape(STEP, pages, width)

        @pl.when(m == 0)
        def _():
            first[...] = total[0]

        position = base + lax.broadcasted_iota(jnp.int32, (STEP, pages, width), 0)
        valid = position.astype(jnp.float32) < bound[...][None]
        total = jnp.where(valid, total, first[...][None])
        emb[pl.ds(pl.multiple_of(m * rows, rows), rows), :] = total.astype(jnp.bfloat16).reshape(rows, width)

    turns = patches // STEP

    def decode_steps(start, stop):
        start, stop = min(start, turns), min(stop, turns)
        if stop > start:
            lax.fori_loop(start, stop, lambda m, carry: (decode(m), carry)[1], 0)

    def shard_at(block, where):
        return qbuf.at[block, core, pl.ds(pl.multiple_of(where * rows_q, rows_q), rows_q), :]

    decode_steps(0, AHEAD)
    loads[2].wait()
    pl.semaphore_wait(barrier, n_pages - 1 + n_blocks - 1)
    z_copies = {
        s: remote(own, own, z_send.at[s], z_recv.at[s], (flip(z, s) * 2 + core, r))
        for s in far_first(nz)
    }
    for copy in z_copies.values():
        copy.start()
    b_copies = {}

    def forward(t):
        if t:
            z_copies[t].wait_recv()
        part = shard_at(r, flip(z, t))
        for s in far_first(n_blocks):
            b_copies[s, t] = remote(
                part, part, b_send.at[s, t], b_recv.at[s, t], (k, flip(r, s))
            )
            b_copies[s, t].start()

    forward(0)
    decode_steps(AHEAD, NEAR)
    for t in range(1, nz // 2 + 1):
        forward(t)
    decode_steps(NEAR, FAR)
    for t in range(nz // 2 + 1, nz):
        forward(t)
    partner = (k + 1 - 2 * core, r)

    def share(s):
        for t in range(nz):
            if s:
                b_copies[s, t].wait_recv()
        half = qbuf.at[flip(r, s), core]
        copy = remote(half, half, c_send.at[s], c_recv.at[s], partner)
        copy.start()
        return copy

    c_copies = {0: share(0)}
    decode_steps(FAR, turns)

    def best_of(source):
        query = qbuf[source].reshape(cols, width)

        best = jnp.full((pages, cols), LOWEST, jnp.float32)
        for m in range(turns):
            sim = lax.dot_general(
                emb[m * rows : (m + 1) * rows, :], query, (((1,), (1,)), ((), ())),
                preferred_element_type=jnp.float32,
            )
            best = jnp.maximum(best, jnp.max(sim.reshape(STEP, pages, cols), axis=0))
        return jnp.where(bound[:, :1] > 0.0, best, LOWEST).astype(jnp.bfloat16)

    c_copies[0].wait_recv()
    income[0] = best_of(r)
    for s in far_first(n_blocks):
        c_copies[s] = share(s)
    d_copies = []
    for s in far_first(n_blocks):
        c_copies[s].wait_recv()
        source = flip(r, s)
        outgo[s] = best_of(source)
        copy = remote(outgo.at[s], income.at[s], d_send.at[s], d_recv.at[s], (k, source))
        copy.start()
        d_copies.append(copy)

    slots = cand.shape[0]
    used = lax.broadcasted_iota(jnp.int32, (slots, n_query), 0) < live[...]
    chosen = cand[...]

    highest = income[0].astype(jnp.float32)
    for copy in d_copies:
        copy.wait_recv()
    for s in range(1, n_blocks):
        highest = jnp.maximum(highest, income[s].astype(jnp.float32))
    sums = lax.dot_general(
        highest.astype(jnp.bfloat16), gather[...], (((1,), (1,)), ((), ())),
        preferred_element_type=jnp.float32,
    )
    picked = jnp.zeros((slots, n_query), jnp.float32)
    for n in range(pages):
        picked = jnp.where(chosen == n, sums[n : n + 1, :], picked)
    picked = jnp.where(used, picked, 0.0)
    wide_q = scoreT.shape[0]
    padded = picked
    if wide_q > n_query:
        padded = jnp.concatenate([padded, jnp.zeros((slots, wide_q - n_query), jnp.float32)], axis=1)
    full = jnp.concatenate([padded, jnp.zeros((width - slots, wide_q), jnp.float32)], axis=0)
    scoreT[...] = full.T

    e_copies = []
    for s in range(n_pages - 1, -1, -1):
        to = flip(k, s)
        values = scoreT[pl.ds((to * n_blocks + r) * per_dev, per_dev), :]
        if s == 0:
            landed[k] = values
        else:
            piece[s] = values
            copy = remote(piece.at[s], landed.at[k], e_send.at[s], e_recv.at[s], (to, r))
            copy.start()
            e_copies.append(copy)
    for copy in e_copies:
        copy.wait_recv()
    for g in range(n_pages):
        arrived = landed[g]
        for i in range(per_dev):
            out_ref[i, g : g + 1, :] = arrived[i : i + 1, :slots]
    started = [*z_copies.values(), *b_copies.values(), *c_copies.values(), *d_copies, *e_copies]
    for copy in started:
        copy.wait_send()


def on_device(queries, centroids, basis, patch_ids, coeffs, page_counts, cand_ids, cand_counts):
    n_pages = lax.axis_size("pages")
    n_blocks = lax.axis_size("blocks")
    owned, qtok, width = queries.shape
    cents, rank, _ = basis.shape
    _, pages, patches = patch_ids.shape
    _, n_query, slots = cand_ids.shape
    rows_q = owned * qtok
    cols = n_pages * rows_q
    args = (
        queries.reshape(rows_q, width),
        centroids,
        basis.reshape(cents * rank, width),
        patch_ids[0],
        coeffs[0],
        page_counts,
        jnp.swapaxes(cand_ids[0], 0, 1),
        cand_counts,
    )
    dma = pltpu.SemaphoreType.DMA
    bf16, f32 = jnp.bfloat16, jnp.float32
    vmem = pltpu.VMEM
    totals = pl.pallas_call(
        functools.partial(kernel, n_pages, n_blocks, qtok),
        out_shape=jax.ShapeDtypeStruct((owned, n_pages, slots), f32),
        in_specs=[pl.BlockSpec(memory_space=pl.ANY)] * len(args),
        out_specs=pl.BlockSpec(memory_space=pltpu.VMEM),
        scratch_shapes=[vmem(a.shape, a.dtype) for a in args[1:]]
        + [
            vmem((n_blocks, 2, cols // 2, width), bf16),
            vmem((patches, pages, width), bf16),
            vmem((patches, pages, width), bf16),
            vmem((patches * pages, width), bf16),
            vmem((pages, width), f32),
            vmem((pages, width), f32),
            vmem((n_blocks, pages, cols), bf16),
            vmem((n_blocks, pages, cols), bf16),
            vmem((n_query, cols), bf16),
            vmem((-(-n_query // 128) * 128, width), f32),
            vmem((n_pages, owned, width), f32),
            vmem((n_pages, owned, width), f32),
            dma((len(args),)),
            dma((n_pages,)), dma((n_pages,)),
            dma((n_blocks, n_pages // 2)), dma((n_blocks, n_pages // 2)),
            dma((n_blocks,)), dma((n_blocks,)),
            dma((n_blocks,)), dma((n_blocks,)),
            dma((n_pages,)), dma((n_pages,)),
        ],
        compiler_params=pltpu.CompilerParams(collective_id=0, has_side_effects=True),
    )(*args)
    return totals / qtok


def solution(mesh):
    placed = (
        P(("pages", "blocks"), None, None),
        P(),
        P(),
        P("pages", None, "blocks"),
        P("pages", None, "blocks"),
        P("pages", None),
        P("pages", None, None),
        P("pages", None),
    )
    return jax.shard_map(
        on_device,
        mesh=mesh,
        in_specs=placed,
        out_specs=P(("pages", "blocks"), None, None),
        check_vma=False,
    )
```
